32 devices in a mesh: slab: 4 (over y, core), bl: 8 (over z, x).
Axes of the slice: x: 2, y: 2, z: 4, core: 2. Of those that a mesh axis runs over, the one named last changes fastest.
Arguments:
- model_image: float32 [2, 8192, 8192], P(None, 'slab', 'bl'), may hold values from -6 to 6
- vis_coords: float32 [512, 2, 128], P(('slab', 'bl')), may hold values from 0 to 32
- vis_observed: float32 [512, 2, 128], P(('slab', 'bl')), may hold values from -6 to 6
- tile_slot: int32 [512], P(('slab', 'bl')), may hold values from 0 to 2047
- tile_group: int32 [512, 1], P(('slab', 'bl')), may hold values from 0 to 7; in each aligned block of 16 rows (0 to 15, 16 to 31, ...) at most 8 rows name the same one
- w_plane: int32 [512], P(('slab', 'bl')), may hold values from 0 to 7
- vis_count: int32 [512], P(('slab', 'bl')), may hold values from 16 to 128, as said below
Outputs:
- residual_image: float32 [2, 8192, 8192], P(None, 'slab', 'bl')
- residual_vis: float32 [512, 2, 128], P(('slab', 'bl'))
The draws below stay inside these ranges and needn't reach their ends.
Inputs may be any that keep to these rules, and one draw needn't show every extreme that they name: `tile_group`: among the 16 subgrids of one device, at most 8 name the same group. `vis_count`: some subgrid holds exactly 128 visibilities.
All inputs are finite; a program needn't handle non-finite values.
Results may differ from the reference program's by a relative error of at most 0.0003.
Values sent between devices are 32-bit elements; how exact they have to be, the bound alone decides.
No kernel may reach another device: no remote copies, remote signals or barrier semaphores. Data moves between devices by JAX's collectives and lax.ppermute only.
A program may use at most 192 MiB of HBM per device.

```python
import math
import jax
import jax.numpy as jnp
import numpy as np
from jax import lax

N = 8192
SUB = 32
NW = 8
VPS = 128
SG_DEV = 16
CAP = 8
NSG = 512
NTILE = 256
TCOLS = 8
N_BL = 8


def draw_vis_count(key, part):
    counts = jax.random.randint(jax.random.fold_in(key, 11), (NSG,), VPS // 8, VPS + 1, dtype=jnp.int32)
    return counts.at[0].set(VPS)


def with_ends(array, rng, smallest, largest):
    spot = [jax.random.randint(jax.random.fold_in(rng, axis), (), 0, length) for axis, length in enumerate(array.shape)]
    widest = array.shape.index(max(array.shape))
    neighbour = spot[:widest] + [(spot[widest] + 1) % array.shape[widest]] + spot[widest + 1:]
    return array.at[tuple(spot)].set(smallest).at[tuple(neighbour)].set(largest)


def shard_levels(rng, extent, shards, smallest, top_value):
    level, own = 1.0, jax.random.fold_in(rng, 6)
    for axis_at, shards_of in shards:
        steps = jnp.exp(jax.random.uniform(jax.random.fold_in(own, axis_at), (shards_of,), jnp.float32, smallest / len(shards), top_value / len(shards)))
        level = level * jnp.repeat(steps, extent[axis_at] // shards_of).reshape([-1 if axis == axis_at else 1 for axis in range(len(extent))])
    return level


def assign_block(key, own, number, rows, amount, top, bound, lean):
    sequence = jax.random.permutation(key, amount)
    heavy_load, usual = shares(amount, rows * top, bound, lean, True), shares(amount, rows * top, bound, lean, False)
    places = jnp.arange(amount)

    def named(lengths, offset_by):
        used = int((lengths > 0).sum())
        fixed = max(1, used // 4)
        passed = fixed + (places - fixed + offset_by * (used - fixed)) % max(1, amount - fixed)
        return jnp.zeros((amount,), jnp.int32).at[sequence[jnp.where(places < fixed, places, passed)]].set(jnp.asarray(lengths, jnp.int32))

    lengths = jnp.where(number % 4 == 0, named(heavy_load, number // 4), named(usual, number - number // 4 - 1))
    mixed = jax.random.permutation(jax.random.fold_in(own, 3), amount)
    giver, receiver = mixed[0:amount // 2 * 2:2], mixed[1:amount // 2 * 2:2]
    margin = jnp.minimum(lengths[giver] - 1, bound - lengths[receiver]) // 2
    margin = jnp.where((giver == sequence[0]) | (receiver == sequence[0]) | (lengths[receiver] == 0), 0, jnp.maximum(margin, 0))
    passed = jax.random.randint(jax.random.fold_in(own, 4), (amount // 2,), 0, 1 << 20) % (margin + 1)
    lengths = lengths.at[giver].add(-passed).at[receiver].add(passed)
    labels = jnp.searchsorted(jnp.cumsum(lengths), jnp.arange(rows * top), side="right").astype(jnp.int32)
    table = labels.reshape(top, rows).T
    table = table[jax.random.permutation(jax.random.fold_in(own, 1), rows)]
    offset_by = jax.random.randint(jax.random.fold_in(own, 2), (rows, 1), 0, top)
    return jnp.take_along_axis(table, (jnp.arange(top)[None, :] + offset_by) % top, axis=1)


def shares(number_of, total, most, lean, full):
    weights = [(1 << 20) // math.isqrt(standing ** lean) + 1 for standing in range(1, number_of + 1)]
    largest = most if full else min(most, max(-(-total // number_of), total * weights[0] // sum(weights)))
    least = 1 if total - largest >= number_of - 1 else 0
    given, spare = [largest] + [least] * (number_of - 1), total - largest - least * (number_of - 1)
    while spare > 0:
        movable = [i for i in range(1, number_of) if given[i] < largest] or [i for i in range(1, number_of) if given[i] < most]
        pool, left = sum([weights[i] for i in movable]), spare
        for i in movable:
            addition = min(most - given[i], max(1, left * weights[i] // pool), spare)
            given[i] = given[i] + addition
            spare = spare - addition
    return np.array(given)


def normal_values(own_key, dims, deviation, reach, cuts=(), held_as=jnp.bfloat16):
    array = jax.random.normal(own_key, dims, jnp.float32) * deviation
    if len(cuts) > 0:
        array = shard_levels(own_key, dims, cuts, -0.22, 0.18) * array
    return jnp.clip(array, min=-reach, max=reach).astype(held_as)


def setup_inputs(seed: int = 0) -> dict:
    seeds = jax.random.split(jax.random.key(seed), 8)
    model_image = normal_values(seeds[0], (2, N, N), 1.0, 6.0, ((1, 4), (2, 8)), jnp.float32)
    vis_coords = jnp.clip(32.0 * jax.random.uniform(seeds[1], (NSG, 2, VPS), jnp.float32) ** shard_levels(seeds[1], (NSG, 2, VPS), ((0, 32),), -0.2, 0.2), 0.0, 32.0)
    vis_observed = normal_values(seeds[2], (NSG, 2, VPS), 1.0, 6.0, ((0, 32),), jnp.float32)
    tile_slot = with_ends(jax.random.randint(seeds[3], (NSG,), 0, NTILE * TCOLS), jax.random.fold_in(seeds[3], 1), 0, (NTILE * TCOLS) - 1).astype(jnp.int32)
    tile_group_keys = jax.random.split(jax.random.fold_in(seeds[4], 1), NSG // SG_DEV)
    tile_group_turns = jax.random.permutation(jax.random.fold_in(seeds[4], 3), NSG // SG_DEV)
    tile_group = jax.vmap(lambda own, number: assign_block(jax.random.fold_in(seeds[4], 2), own, number, SG_DEV, N_BL, 1, CAP, 2))(tile_group_keys, tile_group_turns).reshape((NSG, 1))
    w_plane = with_ends(jax.random.randint(seeds[5], (NSG,), 0, NW), jax.random.fold_in(seeds[5], 1), 0, NW - 1).astype(jnp.int32)
    vis_count = draw_vis_count(jax.random.fold_in(seeds[7], 71), 0)
    return {"model_image": model_image, "vis_coords": vis_coords, "vis_observed": vis_observed, "tile_slot": tile_slot, "tile_group": tile_group, "w_plane": w_plane, "vis_count": vis_count}


w_step = 0.1


def complex_einsum(form, left, right):
    product = lambda first, second: jnp.einsum(form, first, second, precision=lax.Precision.HIGHEST)
    return (product(left[0], right[0]) - product(left[1], right[1]),
            product(left[0], right[1]) + product(left[1], right[0]))


def complex_mul(left, right):
    return (left[0] * right[0] - left[1] * right[1], left[0] * right[1] + left[1] * right[0])


def subgrid_pass(tile_real, tile_imag, coords, observed, planes, counts):
    width = tile_real.shape[-1]
    half = width // 2
    slots = coords.shape[-1]
    index = jnp.arange(width, dtype=jnp.int32)
    offsets = (index - half).astype(jnp.float32)
    turns = (index[:, None] * (index[None, :] - half)) % width
    angle = (2.0 * math.pi / width) * turns.astype(jnp.float32)
    forward_d = (jnp.cos(angle), jnp.sin(angle))
    backward_d = (forward_d[0], -forward_d[1])
    scale_sub = 1.0 / (width * width)
    halfway = complex_einsum('il,kij->klj', forward_d, (tile_real, tile_imag))
    image_sub = complex_einsum('klj,jm->klm', halfway, forward_d)
    image_sub = (image_sub[0] * scale_sub, image_sub[1] * scale_sub)
    radius = (offsets[:, None] ** 2 + offsets[None, :] ** 2) / (half * half)
    phase = -w_step * planes.astype(jnp.float32)[:, None, None] * radius[None]
    screen = (jnp.cos(phase), jnp.sin(phase))
    weighted = complex_mul(screen, image_sub)
    along_a = (-2.0 * math.pi / width) * coords[:, 0, :][:, None, :] * offsets[None, :, None]
    along_b = (-2.0 * math.pi / width) * coords[:, 1, :][:, None, :] * offsets[None, :, None]
    phase_a = (jnp.cos(along_a), jnp.sin(along_a))
    phase_b = (jnp.cos(along_b), jnp.sin(along_b))
    partial_rows = complex_einsum('klm,kmj->klj', weighted, phase_b)
    terms = complex_mul(phase_a, partial_rows)
    predicted = (jnp.sum(terms[0], axis=1), jnp.sum(terms[1], axis=1))
    live = (jnp.arange(slots, dtype=jnp.int32)[None, :] < counts[:, None]).astype(jnp.float32)
    resid_real = (observed[:, 0, :] - predicted[0]) * live
    resid_imag = (observed[:, 1, :] - predicted[1]) * live
    spread = complex_mul((phase_a[0], -phase_a[1]), (resid_real[:, None, :], resid_imag[:, None, :]))
    collected = complex_einsum('klj,kmj->klm', spread, (phase_b[0], -phase_b[1]))
    unscreened = complex_mul((screen[0], -screen[1]), collected)
    middle = complex_einsum('il,klm->kim', backward_d, unscreened)
    tile_out = complex_einsum('kim,jm->kij', middle, backward_d)
    return (jnp.stack([resid_real, resid_imag], axis=1),
            jnp.stack([tile_out[0] * scale_sub, tile_out[1] * scale_sub], axis=1))


def reference(model_image, vis_coords, vis_observed, tile_slot, tile_group, w_plane, vis_count):
    image = lax.complex(model_image[0], model_image[1])
    grid = jnp.fft.fft2(image) / N
    tiles = grid.reshape(NTILE, SUB, NTILE, SUB).transpose(0, 2, 1, 3).reshape(NTILE * NTILE, SUB, SUB)
    index = jnp.arange(NSG, dtype=jnp.int32)
    band = index // (SG_DEV * N_BL)
    column = (band * N_BL + tile_group[:, 0]) * TCOLS + tile_slot // NTILE
    tile_id = ((tile_slot % NTILE) * NTILE + column).astype(jnp.int32)
    blocks = NSG // SG_DEV

    def one_block(pieces):
        block_ids, block_coords, block_obs, block_planes, block_counts = pieces
        chosen = tiles[block_ids]
        return subgrid_pass(jnp.real(chosen), jnp.imag(chosen), block_coords, block_obs, block_planes, block_counts)

    resid_vis, contrib = lax.map(one_block, (
        tile_id.reshape(blocks, SG_DEV),
        vis_coords.reshape(blocks, SG_DEV, 2, VPS),
        vis_observed.reshape(blocks, SG_DEV, 2, VPS),
        w_plane.reshape(blocks, SG_DEV),
        vis_count.reshape(blocks, SG_DEV)))
    resid_vis = resid_vis.reshape(NSG, 2, VPS)
    contrib = contrib.reshape(NSG, 2 * SUB * SUB)
    summed = jax.ops.segment_sum(contrib, tile_id, num_segments=NTILE * NTILE)
    resid_grid = summed.reshape(NTILE, NTILE, 2, SUB, SUB).transpose(2, 0, 3, 1, 4).reshape(2, N, N)
    back = jnp.fft.ifft2(lax.complex(resid_grid[0], resid_grid[1])) * N
    resid_image = jnp.stack([jnp.real(back), jnp.imag(back)]).astype(jnp.float32)
    return resid_image, resid_vis
```

```python
import math

import jax
import jax.numpy as jnp
from jax import lax
from jax.sharding import PartitionSpec as P

SUB = 32


w_step = 0.1


def complex_einsum(form, left, right):
    product = lambda first, second: jnp.einsum(form, first, second, precision=lax.Precision.HIGHEST)
    return (
        product(left[0], right[0]) - product(left[1], right[1]),
        product(left[0], right[1]) + product(left[1], right[0]),
    )


def complex_mul(left, right):
    return (left[0] * right[0] - left[1] * right[1], left[0] * right[1] + left[1] * right[0])


def subgrid_pass(tile_real, tile_imag, coords, observed, planes, counts):
    width = tile_real.shape[-1]
    half = width // 2
    slots = coords.shape[-1]
    index = jnp.arange(width, dtype=jnp.int32)
    offsets = (index - half).astype(jnp.float32)
    turns = index[:, None] * (index[None, :] - half) % width
    angle = 2.0 * math.pi / width * turns.astype(jnp.float32)
    forward_d = (jnp.cos(angle), jnp.sin(angle))
    backward_d = (forward_d[0], -forward_d[1])
    scale_sub = 1.0 / (width * width)
    halfway = complex_einsum("il,kij->klj", forward_d, (tile_real, tile_imag))
    image_sub = complex_einsum("klj,jm->klm", halfway, forward_d)
    image_sub = (image_sub[0] * scale_sub, image_sub[1] * scale_sub)
    radius = (offsets[:, None] ** 2 + offsets[None, :] ** 2) / (half * half)
    phase = -w_step * planes.astype(jnp.float32)[:, None, None] * radius[None]
    screen = (jnp.cos(phase), jnp.sin(phase))
    weighted = complex_mul(screen, image_sub)
    along_a = -2.0 * math.pi / width * coords[:, 0, :][:, None, :] * offsets[None, :, None]
    along_b = -2.0 * math.pi / width * coords[:, 1, :][:, None, :] * offsets[None, :, None]
    phase_a = (jnp.cos(along_a), jnp.sin(along_a))
    phase_b = (jnp.cos(along_b), jnp.sin(along_b))
    partial_rows = complex_einsum("klm,kmj->klj", weighted, phase_b)
    terms = complex_mul(phase_a, partial_rows)
    predicted = (jnp.sum(terms[0], axis=1), jnp.sum(terms[1], axis=1))
    live = (jnp.arange(slots, dtype=jnp.int32)[None, :] < counts[:, None]).astype(jnp.float32)
    resid_real = (observed[:, 0, :] - predicted[0]) * live
    resid_imag = (observed[:, 1, :] - predicted[1]) * live
    spread = complex_mul(
        (phase_a[0], -phase_a[1]), (resid_real[:, None, :], resid_imag[:, None, :])
    )
    collected = complex_einsum("klj,kmj->klm", spread, (phase_b[0], -phase_b[1]))
    unscreened = complex_mul((screen[0], -screen[1]), collected)
    middle = complex_einsum("il,klm->kim", backward_d, unscreened)
    tile_out = complex_einsum("kim,jm->kij", middle, backward_d)
    return (
        jnp.stack([resid_real, resid_imag], axis=1),
        jnp.stack([tile_out[0] * scale_sub, tile_out[1] * scale_sub], axis=1),
    )


def table(product, modulus, sign):
    angle = 2.0 * math.pi / modulus * (product % modulus).astype(jnp.float32)
    return jnp.cos(angle), sign * jnp.sin(angle)


def real_form(pair):
    return jnp.stack([jnp.stack([pair[0], -pair[1]], axis=1), jnp.stack([pair[1], pair[0]], axis=1)], axis=0)


def product_high(form, left, right):
    return jnp.einsum(form, left, right, precision=lax.Precision.HIGH)


def twist(pair, values):
    return jnp.stack(complex_mul(pair, (values[0], values[1])))


def per_device(model_image, vis_coords, vis_observed, tile_slot, tile_group, w_plane, vis_count):
    groups = lax.axis_size("bl")
    bands = lax.axis_size("slab")
    both = ("slab", "bl")
    width_in = model_image.shape[2]
    extent = model_image.shape[1] * bands
    tile_rows = extent // SUB
    owned_cols = tile_rows // (groups * bands)
    sub_count = tile_slot.shape[0]

    tile_u = tile_slot % tile_rows
    tile_v = (lax.axis_index("slab") * groups + tile_group[:, 0]) * owned_cols + tile_slot // tile_rows
    ids = lax.all_gather(tile_u * tile_rows + tile_v, both, axis=0, tiled=True)
    all_u = ids // tile_rows
    all_v = ids % tile_rows

    image = lax.all_to_all(model_image, "slab", split_axis=2, concat_axis=1, tiled=True)
    cols = image.shape[2]
    col = lax.axis_index("bl") * width_in + lax.axis_index("slab") * cols + jnp.arange(cols, dtype=jnp.int32)
    short = jnp.arange(SUB, dtype=jnp.int32)
    long = jnp.arange(tile_rows, dtype=jnp.int32)

    coarse = table(short[:, None] * short[None, :], SUB, -1.0)
    fine = table(short[:, None] * long[None, :], extent, -1.0)
    pick_u = table(all_u[:, None] * long[None, :], tile_rows, -1.0)
    shift_v = table(all_v[:, None] * col[None, :], tile_rows, -1.0)
    inside_v = table(short[:, None] * col[None, :], extent, -1.0)
    conj = lambda pair: (pair[0], -pair[1])
    lift_fine = lambda pair: (pair[0][:, :, None], pair[1][:, :, None])
    lift_v = lambda pair: (pair[0][:, None, :], pair[1][:, None, :])

    stage = product_high("aibq,bqpc->aipc", real_form(coarse), image.reshape(2, SUB, tile_rows, cols))
    stage = twist(lift_fine(fine), stage)
    strips = product_high("agbp,bipc->agic", real_form(pick_u), stage)
    strips = twist(lift_v(shift_v), strips)
    partial = product_high("ajbc,bgic->gaij", real_form(inside_v), strips) / extent
    mine = lax.psum_scatter(partial.reshape(-1, 2 * SUB * SUB), both, scatter_dimension=0, tiled=True)
    mine = mine.reshape(sub_count, 2, SUB, SUB)
    residual_vis, contrib = subgrid_pass(mine[:, 0], mine[:, 1], vis_coords, vis_observed, w_plane, vis_count)
    every = lax.all_gather(contrib.reshape(sub_count, 2 * SUB * SUB), both, axis=0, tiled=True)
    every = every.reshape(-1, 2, SUB, SUB)
    spread = product_high("ajbc,gaij->bgic", real_form(inside_v), every)
    spread = twist(lift_v(conj(shift_v)), spread)
    back = product_high("agbp,agic->bipc", real_form(pick_u), spread)
    back = twist(lift_fine(conj(fine)), back) / extent
    rows = product_high("aibq,aipc->bqpc", real_form(coarse), back)
    residual_image = lax.all_to_all(
        rows.reshape(2, extent, cols), "slab", split_axis=1, concat_axis=2, tiled=True
    )
    return (residual_image, residual_vis)


def solution(mesh):
    placed = (
        P(None, "slab", "bl"),
        P(("slab", "bl"), None, None),
        P(("slab", "bl"), None, None),
        P(("slab", "bl")),
        P(("slab", "bl"), None),
        P(("slab", "bl")),
        P(("slab", "bl")),
    )
    return jax.shard_map(
        per_device,
        mesh=mesh,
        in_specs=placed,
        out_specs=(P(None, "slab", "bl"), P(("slab", "bl"), None, None)),
        check_vma=False,
    )
```
